512 devices in a mesh: dp: 16 (over z), expert: 32 (over x, y, core).
Axes of the slice: x: 4, y: 4, z: 16, core: 2. Of those that a mesh axis runs over, the one named last changes fastest.
Arguments:
- tokens: bfloat16 [4096, 4096], P('expert', 'dp'), may hold values from -6 to 6
- route_ids: int32 [4096, 8], P('expert'), may hold values from 0 to 31, all different within a row; in each aligned block of 128 rows (0 to 127, 128 to 255, ...) at most 40 rows name the same one
- route_weights: bfloat16 [4096, 8], P('expert'), may hold values from 0.099609375 to 0.3984375
- gate_weight: bfloat16 [32, 4096, 768], P('expert', 'dp'), may hold values from -0.09375 to 0.09375
- up_weight: bfloat16 [32, 4096, 768], P('expert', 'dp'), may hold values from -0.09375 to 0.09375
- down_weight: bfloat16 [32, 768, 4096], P('expert', None, 'dp'), may hold values from -0.21875 to 0.21875
- out_grad: bfloat16 [4096, 4096], P('expert', 'dp'), may hold values from -3 to 3
Outputs:
- mixed: bfloat16 [4096, 4096], P('expert', 'dp')
- input_grad: bfloat16 [4096, 4096], P('expert', 'dp')
- gate_weight_grad: float32 [32, 4096, 768], P('expert', 'dp')
- up_weight_grad: float32 [32, 4096, 768], P('expert', 'dp')
- down_weight_grad: float32 [32, 768, 4096], P('expert', None, 'dp')
The draws below stay inside these ranges and needn't reach their ends.
Inputs may be any that keep to these rules, and one draw needn't show every extreme that they name: `route_ids`: each row names 8 different experts. In each aligned block of 128 rows (the tokens of one index of expert) no expert is named by more than 40 rows, a bound that some block reaches.
All inputs are finite; a program needn't handle non-finite values.
Results may differ from the reference program's by a relative error of at most 0.039.
Values may be sent and summed in bfloat16 or wider, within the bound.
A program may use at most 64 MiB of HBM per device.

```python
import math
import jax
import jax.numpy as jnp
import numpy as np
from jax import lax

D = 4096
FW = 768
TOPK = 8
TOK_DEV = 128
EXPERTS = 32
CAP = 40
TOKENS = 4096
N_DP = 16
N_EXPERT = 32


def steps_of(own_key, shape, split, least, top_value):
    level = 1.0
    for axis_at, parts in split:
        heights = jax.random.uniform(jax.random.fold_in(jax.random.fold_in(own_key, 6), axis_at), (parts,), jnp.float32, least / len(split), top_value / len(split))
        level = level * jnp.repeat(jnp.exp(heights), shape[axis_at] // parts).reshape((-1,) + (1,) * (len(shape) - 1 - axis_at))
    return level


def routed_block(key, own, number, rows, amount, top, limit, skew):
    order = jax.random.permutation(key, amount)
    crowded, usual = portions_of(amount, rows * top, limit, skew, True), portions_of(amount, rows * top, limit, skew, False)
    places = jnp.arange(amount)

    def named(tallies, turn):
        used = int((tallies > 0).sum())
        fixed = max(1, used // 4)
        shifted = fixed + (places - fixed + turn * (used - fixed)) % max(1, amount - fixed)
        return jnp.zeros((amount,), jnp.int32).at[order[jnp.where(places < fixed, places, shifted)]].set(jnp.asarray(tallies, jnp.int32))

    tallies = jnp.where(number % 4 == 0, named(crowded, number // 4), named(usual, number - number // 4 - 1))
    mixed = jax.random.permutation(jax.random.fold_in(own, 3), amount)
    donor, taker = mixed[0:amount // 2 * 2:2], mixed[1:amount // 2 * 2:2]
    room = jnp.minimum(tallies[donor] - 1, limit - tallies[taker]) // 2
    room = jnp.where((donor == order[0]) | (taker == order[0]) | (tallies[taker] == 0), 0, jnp.maximum(room, 0))
    shifted = jax.random.randint(jax.random.fold_in(own, 4), (amount // 2,), 0, 1 << 20) % (room + 1)
    tallies = tallies.at[donor].add(-shifted).at[taker].add(shifted)
    members = jnp.searchsorted(jnp.cumsum(tallies), jnp.arange(rows * top), side="right").astype(jnp.int32)
    table = members.reshape(top, rows).T
    table = table[jax.random.permutation(jax.random.fold_in(own, 1), rows)]
    turn = jax.random.randint(jax.random.fold_in(own, 2), (rows, 1), 0, top)
    return jnp.take_along_axis(table, (jnp.arange(top)[None, :] + turn) % top, axis=1)


def portions_of(count, total, bound, lean, full):
    weights = [(1 << 20) // math.isqrt(rank ** lean) + 1 for rank in range(1, count + 1)]
    largest = bound if full else min(bound, max(-(-total // count), total * weights[0] // sum(weights)))
    least = 1 if total - largest >= count - 1 else 0
    counts, rest = [largest] + [least] * (count - 1), total - largest - least * (count - 1)
    while rest > 0:
        free = [i for i in range(1, count) if counts[i] < largest] or [i for i in range(1, count) if counts[i] < bound]
        mass, left = sum([weights[i] for i in free]), rest
        for i in free:
            extra = min(bound - counts[i], max(1, left * weights[i] // mass), rest)
            counts[i] = counts[i] + extra
            rest = rest - extra
    return np.array(counts)


def bell_draw(stream_key, extent, deviation, bound, shards=(), kind=jnp.bfloat16):
    loudness = steps_of(stream_key, extent, shards, -0.22, 0.18) if shards else 1.0
    drawn = jax.random.normal(stream_key, extent, jnp.float32) * deviation * loudness
    return jnp.minimum(jnp.maximum(drawn, -bound), bound).astype(kind)


def setup_inputs(seed: int = 0) -> dict:
    keys = jax.random.split(jax.random.key(seed), 8)
    tokens = bell_draw(keys[0], (TOKENS, D), 1.0, 6.0, ((0, 32), (1, 16)))
    route_ids_keys = jax.random.split(jax.random.fold_in(keys[1], 1), TOKENS // TOK_DEV)
    route_ids_turns = jax.random.permutation(jax.random.fold_in(keys[1], 3), TOKENS // TOK_DEV)
    route_ids = jax.vmap(lambda own, number: routed_block(jax.random.fold_in(keys[1], 2), own, number, TOK_DEV, EXPERTS, TOPK, CAP, 2))(route_ids_keys, route_ids_turns).reshape((TOKENS, TOPK))
    route_weights = jnp.clip(0.099609375 + 0.29882812 * jax.random.uniform(keys[2], (TOKENS, TOPK), jnp.float32) ** steps_of(keys[2], (TOKENS, TOPK), ((0, 32),), -0.2, 0.2), 0.099609375, 0.3984375).astype(jnp.bfloat16)
    gate_weight = bell_draw(keys[3], (EXPERTS, D, FW), D ** -0.5, 0.09375, ((0, 32), (1, 16)))
    up_weight = bell_draw(keys[4], (EXPERTS, D, FW), D ** -0.5, 0.09375, ((0, 32), (1, 16)))
    down_weight = bell_draw(keys[5], (EXPERTS, FW, D), FW ** -0.5, 0.21875, ((0, 32), (2, 16)))
    out_grad = bell_draw(keys[6], (TOKENS, D), 0.5, 3.0, ((0, 32), (1, 16)))
    return {"tokens": tokens, "route_ids": route_ids, "route_weights": route_weights, "gate_weight": gate_weight, "up_weight": up_weight, "down_weight": down_weight, "out_grad": out_grad}


def route_slots(route_ids):
    labels = jnp.arange(EXPERTS, dtype=jnp.int32)
    per_expert = jnp.sum((route_ids[:, :, None] == labels[None, None, :]).astype(jnp.int32), axis=1)
    before = jnp.cumsum(per_expert, axis=0).astype(jnp.int32) - per_expert
    return jnp.take_along_axis(before, route_ids, axis=1)


def slice_sum(first_op, second_op, form):
    partial_value = jnp.einsum(form, first_op.astype(jnp.float32), second_op.astype(jnp.float32), precision=lax.Precision.HIGHEST)
    rounded = lax.optimization_barrier(partial_value.astype(jnp.bfloat16))
    return jnp.sum(rounded.astype(jnp.float32), axis=0)


def reference(tokens, route_ids, route_weights, gate_weight, up_weight, down_weight, out_grad):
    local_width = D // N_DP
    row_total = N_EXPERT * CAP
    blocks = route_ids.reshape(N_EXPERT, TOK_DEV, TOPK)
    slots = jax.vmap(route_slots)(blocks)
    source = jnp.arange(N_EXPERT, dtype=jnp.int32)[:, None, None]
    dest_row = (source * CAP + slots).reshape(TOKENS, TOPK).astype(jnp.int32)
    token_index = jnp.broadcast_to(jnp.arange(TOKENS, dtype=jnp.int32)[:, None], (TOKENS, TOPK))
    slot_table = jnp.full((EXPERTS, row_total), TOKENS, jnp.int32).at[route_ids, dest_row].set(token_index)
    scale_table = jnp.zeros((EXPERTS, row_total), jnp.float32).at[route_ids, dest_row].set(route_weights.astype(jnp.float32))

    def one_expert(carry, inputs):
        mixed_acc, grad_acc = carry
        weight_g, weight_u, weight_d, slot_tokens, slot_scale = inputs
        present = slot_tokens < TOKENS
        safe_index = jnp.minimum(slot_tokens, TOKENS - 1)
        expert_rows = jnp.where(present[:, None], tokens[safe_index], jnp.zeros((), jnp.bfloat16))
        split_rows = expert_rows.reshape(row_total, N_DP, local_width)
        gate_pre = slice_sum(split_rows, weight_g.reshape(N_DP, local_width, FW), "rpd,pdf->prf")
        up_pre = slice_sum(split_rows, weight_u.reshape(N_DP, local_width, FW), "rpd,pdf->prf")
        hidden = (jax.nn.silu(gate_pre) * up_pre).astype(jnp.bfloat16)
        produced = jnp.dot(hidden, weight_d, preferred_element_type=jnp.float32).astype(jnp.bfloat16)
        weighted_out = lax.optimization_barrier((slot_scale[:, None] * produced.astype(jnp.float32)).astype(jnp.bfloat16))
        grad_rows = jnp.where(present[:, None], out_grad[safe_index], jnp.zeros((), jnp.bfloat16))
        upstream = (slot_scale[:, None] * grad_rows.astype(jnp.float32)).astype(jnp.bfloat16)
        hidden_grad = slice_sum(upstream.reshape(row_total, N_DP, local_width), weight_d.reshape(FW, N_DP, local_width), "rpd,fpd->prf")
        sigmoid_gate = jax.nn.sigmoid(gate_pre)
        gate_delta = (hidden_grad * up_pre * sigmoid_gate * (1.0 + gate_pre * (1.0 - sigmoid_gate))).astype(jnp.bfloat16)
        up_delta = (hidden_grad * jax.nn.silu(gate_pre)).astype(jnp.bfloat16)
        down_grad = jnp.dot(hidden.T, upstream, preferred_element_type=jnp.float32)
        gate_grad = jnp.dot(expert_rows.T, gate_delta, preferred_element_type=jnp.float32)
        up_grad = jnp.dot(expert_rows.T, up_delta, preferred_element_type=jnp.float32)
        back_rows = (jnp.dot(gate_delta, weight_g.T, preferred_element_type=jnp.float32) + jnp.dot(up_delta, weight_u.T, preferred_element_type=jnp.float32)).astype(jnp.bfloat16)
        drop_at = jnp.where(present, slot_tokens, TOKENS).astype(jnp.int32)
        mixed_acc = mixed_acc.at[drop_at].add(weighted_out.astype(jnp.float32), mode="drop")
        grad_acc = grad_acc.at[drop_at].add(back_rows.astype(jnp.float32), mode="drop")
        return (mixed_acc, grad_acc), (gate_grad, up_grad, down_grad)

    start = (jnp.zeros((TOKENS, D), jnp.float32), jnp.zeros((TOKENS, D), jnp.float32))
    (mixed_acc, grad_acc), (gate_grads, up_grads, down_grads) = lax.scan(one_expert, start, (gate_weight, up_weight, down_weight, slot_table, scale_table))
    return (mixed_acc.astype(jnp.bfloat16), grad_acc.astype(jnp.bfloat16), gate_grads, up_grads, down_grads)
```

```python
import jax
import jax.numpy as jnp
from jax import lax
from jax.sharding import PartitionSpec as P

SLOT_CHUNKS = (40,)


def dot_of(first_op, second_op, first_dim, second_dim):
    return lax.dot_general(
        first_op,
        second_op,
        (((first_dim,), (second_dim,)), ((), ())),
        preferred_element_type=jnp.float32,
    )


def slot_matrices(route_ids, route_weights, expert_count, capacity):
    tok_count = route_ids.shape[0]
    labels = lax.broadcasted_iota(jnp.int32, (expert_count, 1, 1), 0)
    named = route_ids.T[None, :, :] == labels
    hit = jnp.any(named, axis=1)
    weight = jnp.sum(jnp.where(named, route_weights.astype(jnp.float32).T[None], 0.0), axis=1)
    earlier = lax.broadcasted_iota(jnp.int32, (tok_count, tok_count), 0)
    later = lax.broadcasted_iota(jnp.int32, (tok_count, tok_count), 1)
    before = (earlier < later).astype(jnp.bfloat16)
    rank = dot_of(hit.astype(jnp.bfloat16), before, 1, 0).astype(jnp.int32)
    rank = jnp.where(hit, rank, -1)
    slots = lax.broadcasted_iota(jnp.int32, (expert_count, capacity, tok_count), 1)
    taken = rank[:, None, :] == slots
    place = jnp.where(taken, 1.0, 0.0).astype(jnp.bfloat16)
    scale = jnp.where(taken, weight[:, None, :], 0.0).astype(jnp.bfloat16)
    return place, scale


def swap(rows):
    return lax.all_to_all(rows, "expert", split_axis=0, concat_axis=0, tiled=True)


def pointwise(gate_pre, up_pre, hidden_grad):
    sigmoid_gate = jax.nn.sigmoid(gate_pre)
    silu_gate = gate_pre * sigmoid_gate
    hidden = (silu_gate * up_pre).astype(jnp.bfloat16)
    gate_delta = (
        hidden_grad * up_pre * sigmoid_gate * (1.0 + gate_pre * (1.0 - sigmoid_gate))
    ).astype(jnp.bfloat16)
    up_delta = (hidden_grad * silu_gate).astype(jnp.bfloat16)
    return hidden, gate_delta, up_delta


def shards(tokens, route_ids, route_weights, gate_weight, up_weight, down_weight, out_grad):
    expert_count = lax.axis_size("expert")
    tok_count, width = tokens.shape
    top_count = route_ids.shape[1]
    capacity = min(tok_count, tok_count * top_count // expert_count + tok_count // 16)
    weight_g, weight_u, weight_d = gate_weight[0], up_weight[0], down_weight[0]
    place, scale = slot_matrices(route_ids, route_weights, expert_count, capacity)
    chunks, start = [], 0
    for size in SLOT_CHUNKS:
        chunks.append(
            tuple(
                m[:, start : start + size].reshape(expert_count * size, tok_count)
                for m in (place, scale)
            )
        )
        start += size
    assert start == capacity
    sent = []
    for place_c, scale_c in chunks:
        sent.append(
            swap(
                jnp.concatenate(
                    [
                        dot_of(place_c, tokens, 1, 0).astype(jnp.bfloat16),
                        dot_of(scale_c, out_grad, 1, 0).astype(jnp.bfloat16),
                    ],
                    axis=1,
                )
            )
        )
    parts, after = [], None
    for got in sent:
        if after is not None and False:
            got, after = lax.optimization_barrier((got, after))
            parts[-1] = parts[-1][:3] + after
        rows, upstream = got[:, :width], got[:, width:]
        partial = (
            dot_of(rows, weight_g, 1, 0).astype(jnp.bfloat16),
            dot_of(rows, weight_u, 1, 0).astype(jnp.bfloat16),
            dot_of(upstream, weight_d, 1, 1).astype(jnp.bfloat16),
        )
        after = lax.psum(partial, "dp")
        parts.append((rows, upstream, None) + tuple(after))
    mixed = input_grad = gate_grad = up_grad = down_grad = 0.0
    for (place_c, scale_c), (rows, upstream, _, *summed) in zip(chunks, parts):
        hidden, gate_delta, up_delta = pointwise(*(v.astype(jnp.float32) for v in summed))
        produced = dot_of(hidden, weight_d, 1, 0).astype(jnp.bfloat16)
        back_rows = (
            dot_of(gate_delta, weight_g, 1, 1) + dot_of(up_delta, weight_u, 1, 1)
        ).astype(jnp.bfloat16)
        back = swap(jnp.concatenate([produced, back_rows], axis=1))
        mixed += dot_of(scale_c, back[:, :width], 0, 0)
        input_grad += dot_of(place_c, back[:, width:], 0, 0)
        gate_grad += dot_of(rows, gate_delta, 0, 0)
        up_grad += dot_of(rows, up_delta, 0, 0)
        down_grad += dot_of(hidden, upstream, 0, 0)
    return (
        mixed.astype(jnp.bfloat16),
        input_grad.astype(jnp.bfloat16),
        gate_grad[None],
        up_grad[None],
        down_grad[None],
    )


def solution(mesh):
    return jax.shard_map(
        shards,
        mesh=mesh,
        in_specs=(
            P("expert", "dp"),
            P("expert", None),
            P("expert", None),
            P("expert", "dp", None),
            P("expert", "dp", None),
            P("expert", None, "dp"),
            P("expert", "dp"),
        ),
        out_specs=(
            P("expert", "dp"),
            P("expert", "dp"),
            P("expert", "dp", None),
            P("expert", "dp", None),
            P("expert", None, "dp"),
        ),
        check_vma=False,
    )
```

```python
import functools

import jax
import jax.numpy as jnp
from jax import lax
from jax.experimental import pallas as pl
from jax.experimental.pallas import tpu as pltpu
from jax.sharding import PartitionSpec as P

SLOT_CHUNKS = (40,)


def dot_of(first_op, second_op, first_dim, second_dim):
    return lax.dot_general(
        first_op,
        second_op,
        (((first_dim,), (second_dim,)), ((), ())),
        preferred_element_type=jnp.float32,
    )


def slot_matrices(route_ids, route_weights, expert_count, capacity):
    tok_count = route_ids.shape[0]
    labels = lax.broadcasted_iota(jnp.int32, (expert_count, 1, 1), 0)
    named = route_ids.T[None, :, :] == labels
    hit = jnp.any(named, axis=1)
    weight = jnp.sum(jnp.where(named, route_weights.astype(jnp.float32).T[None], 0.0), axis=1)
    earlier = lax.broadcasted_iota(jnp.int32, (tok_count, tok_count), 0)
    later = lax.broadcasted_iota(jnp.int32, (tok_count, tok_count), 1)
    before = (earlier < later).astype(jnp.bfloat16)
    rank = dot_of(hit.astype(jnp.bfloat16), before, 1, 0).astype(jnp.int32)
    rank = jnp.where(hit, rank, -1)
    slots = lax.broadcasted_iota(jnp.int32, (expert_count, capacity, tok_count), 1)
    taken = rank[:, None, :] == slots
    place = jnp.where(taken, 1.0, 0.0).astype(jnp.bfloat16)
    scale = jnp.where(taken, weight[:, None, :], 0.0).astype(jnp.bfloat16)
    return place, scale


def swap(rows):
    return lax.all_to_all(rows, "expert", split_axis=0, concat_axis=0, tiled=True)


def pointwise(gate_pre, up_pre, hidden_grad):
    sigmoid_gate = jax.nn.sigmoid(gate_pre)
    silu_gate = gate_pre * sigmoid_gate
    hidden = (silu_gate * up_pre).astype(jnp.bfloat16)
    gate_delta = (
        hidden_grad * up_pre * sigmoid_gate * (1.0 + gate_pre * (1.0 - sigmoid_gate))
    ).astype(jnp.bfloat16)
    up_delta = (hidden_grad * silu_gate).astype(jnp.bfloat16)
    return hidden, gate_delta, up_delta


def ring_kernel(ring, *refs):
    partials, outs = refs[:3], refs[3:6]
    landed, sum_send, sum_recv, own_send, own_recv = refs[6:]
    rows, units = partials[0].shape[0] // ring, partials[0].shape[1]
    half = units // 2
    me = lax.axis_index("dp")
    peers = (lax.rem(me + 1, ring), lax.rem(me + ring - 1, ring))
    streams = [(way, a) for a in range(3) for way in range(2)]

    def block(ref, index, way):
        at = lax.rem(index + 2 * ring, ring)
        return ref.at[pl.ds(pl.multiple_of(at * rows, rows), rows), pl.ds(way * half, half)]

    def dest(step, way):
        return me - 1 - step if way == 0 else me + 1 + step

    def sum_copy(step, way, a, first=False):
        k = 2 * a + way
        source = block(partials[a], dest(0, way), way) if first else landed.at[step - 1, k]
        return pltpu.make_async_remote_copy(
            src_ref=source,
            dst_ref=landed.at[step, k],
            send_sem=sum_send.at[step, k],
            recv_sem=sum_recv.at[step, k],
            device_id={"dp": peers[way]},
            device_id_type=pl.DeviceIdType.MESH,
        )

    def own_copy(step, way, a):
        k = 2 * a + way
        place = block(outs[a], me - step if way == 0 else me + step, way)
        return pltpu.make_async_remote_copy(
            src_ref=place,
            dst_ref=place,
            send_sem=own_send.at[step, k],
            recv_sem=own_recv.at[step, k],
            device_id={"dp": peers[way]},
            device_id_type=pl.DeviceIdType.MESH,
        )

    def own_arrival(step, way, a):
        k = 2 * a + way
        place = block(outs[a], me - 1 - step if way == 0 else me + 1 + step, way)
        return pltpu.make_async_remote_copy(
            src_ref=place,
            dst_ref=place,
            send_sem=own_send.at[step, k],
            recv_sem=own_recv.at[step, k],
            device_id={"dp": peers[way]},
            device_id_type=pl.DeviceIdType.MESH,
        )

    def total(step, way, a):
        mine = block(partials[a], dest(step + 1, way), way)[...].astype(jnp.float32)
        return landed[step, 2 * a + way].astype(jnp.float32) + mine

    barrier = pltpu.get_barrier_semaphore()
    for peer in peers:
        pl.semaphore_signal(
            barrier, inc=1, device_id={"dp": peer}, device_id_type=pl.DeviceIdType.MESH
        )
    pl.semaphore_wait(barrier, 2)

    for way, a in streams:
        sum_copy(0, way, a, True).start()

    def sum_step(step, carry):
        for way, a in streams:
            sum_copy(step, way, a, True).wait_recv()
            landed[step, 2 * a + way] = total(step, way, a).astype(jnp.bfloat16)
            sum_copy(step + 1, way, a).start()
        return carry

    lax.fori_loop(0, ring - 2, sum_step, 0)

    last = ring - 2
    for way in range(2):
        for a in range(3):
            sum_copy(last, way, a, True).wait_recv()
        values = pointwise(*(total(last, way, a) for a in range(3)))
        for a in range(3):
            block(outs[a], me, way)[...] = values[a]
        for a in range(3):
            own_copy(0, way, a).start()

    def own_step(step, carry):
        for way, a in streams:
            own_arrival(step, way, a).wait_recv()
            own_copy(step + 1, way, a).start()
        return carry

    lax.fori_loop(0, ring - 2, own_step, 0)
    for way, a in streams:
        own_arrival(last, way, a).wait_recv()

    def drain(step, carry):
        for way, a in streams:
            sum_copy(step, way, a, True).wait_send()
            own_copy(step, way, a).wait_send()
        return carry

    lax.fori_loop(0, ring - 1, drain, 0)


def reduced_units(partials):
    ring = lax.axis_size("dp")
    rows, units = partials[0].shape
    sems = pltpu.SemaphoreType.DMA((ring - 1, 6))
    return pl.pallas_call(
        functools.partial(ring_kernel, ring),
        out_shape=[jax.ShapeDtypeStruct((rows, units), jnp.bfloat16)] * 3,
        in_specs=[pl.BlockSpec(memory_space=pltpu.VMEM)] * 3,
        out_specs=[pl.BlockSpec(memory_space=pltpu.VMEM)] * 3,
        scratch_shapes=[
            pltpu.VMEM((ring - 1, 6, rows // ring, units // 2), jnp.bfloat16),
            sems,
            sems,
            sems,
            sems,
        ],
        compiler_params=pltpu.CompilerParams(
            collective_id=0, has_side_effects=True, vmem_limit_bytes=48 * 1024 * 1024
        ),
    )(*partials)


def shards(tokens, route_ids, route_weights, gate_weight, up_weight, down_weight, out_grad):
    expert_count = lax.axis_size("expert")
    tok_count, width = tokens.shape
    top_count = route_ids.shape[1]
    capacity = min(tok_count, tok_count * top_count // expert_count + tok_count // 16)
    weight_g, weight_u, weight_d = gate_weight[0], up_weight[0], down_weight[0]
    place, scale = slot_matrices(route_ids, route_weights, expert_count, capacity)
    chunks, start = [], 0
    for size in SLOT_CHUNKS:
        chunks.append(
            tuple(
                m[:, start : start + size].reshape(expert_count * size, tok_count)
                for m in (place, scale)
            )
        )
        start += size
    assert start == capacity
    sent = []
    for place_c, scale_c in chunks:
        sent.append(
            swap(
                jnp.concatenate(
                    [
                        dot_of(place_c, tokens, 1, 0).astype(jnp.bfloat16),
                        dot_of(scale_c, out_grad, 1, 0).astype(jnp.bfloat16),
                    ],
                    axis=1,
                )
            )
        )
    parts, after = [], None
    for got in sent:
        if after is not None and False:
            got, after = lax.optimization_barrier((got, after))
            parts[-1] = parts[-1][:3] + after
        rows, upstream = got[:, :width], got[:, width:]
        partial = (
            dot_of(rows, weight_g, 1, 0).astype(jnp.bfloat16),
            dot_of(rows, weight_u, 1, 0).astype(jnp.bfloat16),
            dot_of(upstream, weight_d, 1, 1).astype(jnp.bfloat16),
        )
        after = reduced_units(partial)
        parts.append((rows, upstream, None) + tuple(after))
    mixed = input_grad = gate_grad = up_grad = down_grad = 0.0
    for (place_c, scale_c), (rows, upstream, _, *summed) in zip(chunks, parts):
        hidden, gate_delta, up_delta = summed
        produced = dot_of(hidden, weight_d, 1, 0).astype(jnp.bfloat16)
        back_rows = (
            dot_of(gate_delta, weight_g, 1, 1) + dot_of(up_delta, weight_u, 1, 1)
        ).astype(jnp.bfloat16)
        back = swap(jnp.concatenate([produced, back_rows], axis=1))
        mixed += dot_of(scale_c, back[:, :width], 0, 0)
        input_grad += dot_of(place_c, back[:, width:], 0, 0)
        gate_grad += dot_of(rows, gate_delta, 0, 0)
        up_grad += dot_of(rows, up_delta, 0, 0)
        down_grad += dot_of(hidden, upstream, 0, 0)
    return (
        mixed.astype(jnp.bfloat16),
        input_grad.astype(jnp.bfloat16),
        gate_grad[None],
        up_grad[None],
        down_grad[None],
    )


def solution(mesh):
    return jax.shard_map(
        shards,
        mesh=mesh,
        in_specs=(
            P("expert", "dp"),
            P("expert", None),
            P("expert", None),
            P("expert", "dp", None),
            P("expert", "dp", None),
            P("expert", None, "dp"),
            P("expert", "dp"),
        ),
        out_specs=(
            P("expert", "dp"),
            P("expert", "dp"),
            P("expert", "dp", None),
            P("expert", "dp", None),
            P("expert", None, "dp"),
        ),
        check_vma=False,
    )
```

```python
import functools

import jax
import jax.numpy as jnp
from jax import lax
from jax.experimental import pallas as pl
from jax.experimental.pallas import tpu as pltpu
from jax.sharding import PartitionSpec as P

SLOT_CHUNKS = (24, 16)


def dot_of(first_op, second_op, first_dim, second_dim):
    return lax.dot_general(
        first_op,
        second_op,
        (((first_dim,), (second_dim,)), ((), ())),
        preferred_element_type=jnp.float32,
    )


def slot_matrices(route_ids, route_weights, expert_count, capacity):
    tok_count = route_ids.shape[0]
    labels = lax.broadcasted_iota(jnp.int32, (expert_count, 1, 1), 0)
    named = route_ids.T[None, :, :] == labels
    hit = jnp.any(named, axis=1)
    weight = jnp.sum(jnp.where(named, route_weights.astype(jnp.float32).T[None], 0.0), axis=1)
    earlier = lax.broadcasted_iota(jnp.int32, (tok_count, tok_count), 0)
    later = lax.broadcasted_iota(jnp.int32, (tok_count, tok_count), 1)
    before = (earlier < later).astype(jnp.bfloat16)
    rank = dot_of(hit.astype(jnp.bfloat16), before, 1, 0).astype(jnp.int32)
    rank = jnp.where(hit, rank, -1)
    slots = lax.broadcasted_iota(jnp.int32, (expert_count, capacity, tok_count), 1)
    taken = rank[:, None, :] == slots
    place = jnp.where(taken, 1.0, 0.0).astype(jnp.bfloat16)
    scale = jnp.where(taken, weight[:, None, :], 0.0).astype(jnp.bfloat16)
    return place, scale


def swap(rows):
    return lax.all_to_all(rows, "expert", split_axis=0, concat_axis=0, tiled=True)


def pointwise(gate_pre, up_pre, hidden_grad):
    sigmoid_gate = jax.nn.sigmoid(gate_pre)
    silu_gate = gate_pre * sigmoid_gate
    hidden = (silu_gate * up_pre).astype(jnp.bfloat16)
    gate_delta = (
        hidden_grad * up_pre * sigmoid_gate * (1.0 + gate_pre * (1.0 - sigmoid_gate))
    ).astype(jnp.bfloat16)
    up_delta = (hidden_grad * silu_gate).astype(jnp.bfloat16)
    return hidden, gate_delta, up_delta


def ring_kernel(ring, *refs):
    partials, outs = refs[:3], refs[3:6]
    landed, sum_send, sum_recv, own_send, own_recv = refs[6:]
    rows, units = partials[0].shape[0] // ring, partials[0].shape[1]
    half = units // 2
    me = lax.axis_index("dp")
    peers = (lax.rem(me + 1, ring), lax.rem(me + ring - 1, ring))
    streams = [(way, a) for a in range(3) for way in range(2)]

    def block(ref, index, way):
        at = lax.rem(index + 2 * ring, ring)
        return ref.at[pl.ds(pl.multiple_of(at * rows, rows), rows), pl.ds(way * half, half)]

    def dest(step, way):
        return me - 1 - step if way == 0 else me + 1 + step

    def sum_copy(step, way, a, first=False):
        k = 2 * a + way
        source = block(partials[a], dest(0, way), way) if first else landed.at[step - 1, k]
        return pltpu.make_async_remote_copy(
            src_ref=source,
            dst_ref=landed.at[step, k],
            send_sem=sum_send.at[step, k],
            recv_sem=sum_recv.at[step, k],
            device_id={"dp": peers[way]},
            device_id_type=pl.DeviceIdType.MESH,
        )

    def own_copy(step, way, a):
        k = 2 * a + way
        place = block(outs[a], me - step if way == 0 else me + step, way)
        return pltpu.make_async_remote_copy(
            src_ref=place,
            dst_ref=place,
            send_sem=own_send.at[step, k],
            recv_sem=own_recv.at[step, k],
            device_id={"dp": peers[way]},
            device_id_type=pl.DeviceIdType.MESH,
        )

    def own_arrival(step, way, a):
        k = 2 * a + way
        place = block(outs[a], me - 1 - step if way == 0 else me + 1 + step, way)
        return pltpu.make_async_remote_copy(
            src_ref=place,
            dst_ref=place,
            send_sem=own_send.at[step, k],
            recv_sem=own_recv.at[step, k],
            device_id={"dp": peers[way]},
            device_id_type=pl.DeviceIdType.MESH,
        )

    def total(step, way, a):
        mine = block(partials[a], dest(step + 1, way), way)[...].astype(jnp.float32)
        return landed[step, 2 * a + way].astype(jnp.float32) + mine

    barrier = pltpu.get_barrier_semaphore()
    for peer in peers:
        pl.semaphore_signal(
            barrier, inc=1, device_id={"dp": peer}, device_id_type=pl.DeviceIdType.MESH
        )
    pl.semaphore_wait(barrier, 2)

    for way, a in streams:
        sum_copy(0, way, a, True).start()

    def sum_step(step, carry):
        for way, a in streams:
            sum_copy(step, way, a, True).wait_recv()
            landed[step, 2 * a + way] = total(step, way, a).astype(jnp.bfloat16)
            sum_copy(step + 1, way, a).start()
        return carry

    lax.fori_loop(0, ring - 2, sum_step, 0)

    last = ring - 2
    for way in range(2):
        for a in range(3):
            sum_copy(last, way, a, True).wait_recv()
        values = pointwise(*(total(last, way, a) for a in range(3)))
        for a in range(3):
            block(outs[a], me, way)[...] = values[a]
        for a in range(3):
            own_copy(0, way, a).start()

    def own_step(step, carry):
        for way, a in streams:
            own_arrival(step, way, a).wait_recv()
            own_copy(step + 1, way, a).start()
        return carry

    lax.fori_loop(0, ring - 2, own_step, 0)
    for way, a in streams:
        own_arrival(last, way, a).wait_recv()

    def drain(step, carry):
        for way, a in streams:
            sum_copy(step, way, a, True).wait_send()
            own_copy(step, way, a).wait_send()
        return carry

    lax.fori_loop(0, ring - 1, drain, 0)


def reduced_units(partials, number):
    ring = lax.axis_size("dp")
    rows, units = partials[0].shape
    sems = pltpu.SemaphoreType.DMA((ring - 1, 6))
    return pl.pallas_call(
        functools.partial(ring_kernel, ring),
        out_shape=[jax.ShapeDtypeStruct((rows, units), jnp.bfloat16)] * 3,
        in_specs=[pl.BlockSpec(memory_space=pltpu.VMEM)] * 3,
        out_specs=[pl.BlockSpec(memory_space=pltpu.VMEM)] * 3,
        scratch_shapes=[
            pltpu.VMEM((ring - 1, 6, rows // ring, units // 2), jnp.bfloat16),
            sems,
            sems,
            sems,
            sems,
        ],
        compiler_params=pltpu.CompilerParams(
            collective_id=number, has_side_effects=True, vmem_limit_bytes=48 * 1024 * 1024
        ),
        cost_estimate=pl.CostEstimate(
            flops=40 * rows * units, bytes_accessed=300_000_000, transcendentals=0
        ),
    )(*partials)


def shards(tokens, route_ids, route_weights, gate_weight, up_weight, down_weight, out_grad):
    expert_count = lax.axis_size("expert")
    tok_count, width = tokens.shape
    top_count = route_ids.shape[1]
    capacity = min(tok_count, tok_count * top_count // expert_count + tok_count // 16)
    weight_g, weight_u, weight_d = gate_weight[0], up_weight[0], down_weight[0]
    place, scale = slot_matrices(route_ids, route_weights, expert_count, capacity)
    chunks, start = [], 0
    for size in SLOT_CHUNKS:
        chunks.append(
            tuple(
                m[:, start : start + size].reshape(expert_count * size, tok_count)
                for m in (place, scale)
            )
        )
        start += size
    assert start == capacity
    sent = []
    for place_c, scale_c in chunks:
        sent.append(
            swap(
                jnp.concatenate(
                    [
                        dot_of(place_c, tokens, 1, 0).astype(jnp.bfloat16),
                        dot_of(scale_c, out_grad, 1, 0).astype(jnp.bfloat16),
                    ],
                    axis=1,
                )
            )
        )
    mixed = input_grad = gate_grad = up_grad = down_grad = 0.0
    out = None
    backs, kept = [], []
    for number, got in enumerate(sent):
        if out is not None:
            got, out = lax.optimization_barrier((got, out))
            backs.append(swap(out))
        rows, upstream = got[:, :width], got[:, width:]
        hidden, gate_delta, up_delta = reduced_units(
            (
                dot_of(rows, weight_g, 1, 0).astype(jnp.bfloat16),
                dot_of(rows, weight_u, 1, 0).astype(jnp.bfloat16),
                dot_of(upstream, weight_d, 1, 1).astype(jnp.bfloat16),
            ),
            number,
        )
        produced = dot_of(hidden, weight_d, 1, 0).astype(jnp.bfloat16)
        back_rows = (
            dot_of(gate_delta, weight_g, 1, 1) + dot_of(up_delta, weight_u, 1, 1)
        ).astype(jnp.bfloat16)
        out = jnp.concatenate([produced, back_rows], axis=1)
        kept.append((rows, upstream, hidden, gate_delta, up_delta))
    backs.append(swap(out))
    for (place_c, scale_c), back in zip(chunks, backs):
        mixed += dot_of(scale_c, back[:, :width], 0, 0)
        input_grad += dot_of(place_c, back[:, width:], 0, 0)
    for rows, upstream, hidden, gate_delta, up_delta in kept:
        gate_grad += dot_of(rows, gate_delta, 0, 0)
        up_grad += dot_of(rows, up_delta, 0, 0)
        down_grad += dot_of(hidden, upstream, 0, 0)
    return (
        mixed.astype(jnp.bfloat16),
        input_grad.astype(jnp.bfloat16),
        gate_grad[None],
        up_grad[None],
        down_grad[None],
    )


def solution(mesh):
    return jax.shard_map(
        shards,
        mesh=mesh,
        in_specs=(
            P("expert", "dp"),
            P("expert", None),
            P("expert", None),
            P("expert", "dp", None),
            P("expert", "dp", None),
            P("expert", None, "dp"),
            P("expert", "dp"),
        ),
        out_specs=(
            P("expert", "dp"),
            P("expert", "dp"),
            P("expert", "dp", None),
            P("expert", "dp", None),
            P("expert", None, "dp"),
        ),
        check_vma=False,
    )
```

```python
import functools

import jax
import jax.numpy as jnp
from jax import lax
from jax.experimental import pallas as pl
from jax.experimental.pallas import tpu as pltpu
from jax.sharding import PartitionSpec as P

SLOT_CHUNKS = (40,)


def dot_of(first_op, second_op, first_dim, second_dim):
    return lax.dot_general(
        first_op,
        second_op,
        (((first_dim,), (second_dim,)), ((), ())),
        preferred_element_type=jnp.float32,
    )


def slot_matrices(route_ids, route_weights, expert_count, capacity):
    tok_count = route_ids.shape[0]
    labels = lax.broadcasted_iota(jnp.int32, (expert_count, 1, 1), 0)
    named = route_ids.T[None, :, :] == labels
    hit = jnp.any(named, axis=1)
    weight = jnp.sum(jnp.where(named, route_weights.astype(jnp.float32).T[None], 0.0), axis=1)
    earlier = lax.broadcasted_iota(jnp.int32, (tok_count, tok_count), 0)
    later = lax.broadcasted_iota(jnp.int32, (tok_count, tok_count), 1)
    before = (earlier < later).astype(jnp.bfloat16)
    rank = dot_of(hit.astype(jnp.bfloat16), before, 1, 0).astype(jnp.int32)
    rank = jnp.where(hit, rank, -1)
    slots = lax.broadcasted_iota(jnp.int32, (expert_count, capacity, tok_count), 1)
    taken = rank[:, None, :] == slots
    place = jnp.where(taken, 1.0, 0.0).astype(jnp.bfloat16)
    scale = jnp.where(taken, weight[:, None, :], 0.0).astype(jnp.bfloat16)
    return place, scale


def swap(rows):
    return lax.all_to_all(rows, "expert", split_axis=0, concat_axis=0, tiled=True)


def pointwise(gate_pre, up_pre, hidden_grad):
    sigmoid_gate = jax.nn.sigmoid(gate_pre)
    silu_gate = gate_pre * sigmoid_gate
    hidden = (silu_gate * up_pre).astype(jnp.bfloat16)
    gate_delta = (
        hidden_grad * up_pre * sigmoid_gate * (1.0 + gate_pre * (1.0 - sigmoid_gate))
    ).astype(jnp.bfloat16)
    up_delta = (hidden_grad * silu_gate).astype(jnp.bfloat16)
    return hidden, gate_delta, up_delta


def ring_kernel(ring, *refs):
    partials, outs = refs[:3], refs[3:6]
    landed, sum_send, sum_recv, own_send, own_recv = refs[6:]
    rows = partials[0].shape[0] // ring
    hops = (ring // 2, ring - 1 - ring // 2)
    me = lax.axis_index("dp")
    peers = (lax.rem(me + 1, ring), lax.rem(me + ring - 1, ring))
    streams = [(way, a) for a in range(3) for way in range(2)]

    def block(ref, index, way):
        at = lax.rem(index + 2 * ring, ring)
        return ref.at[pl.ds(pl.multiple_of(at * rows, rows), rows), :]

    def dest(step, way):
        return me + hops[0] - step if way == 0 else me - hops[1] + step

    def sum_copy(step, way, a, first=False):
        k = 2 * a + way
        source = block(partials[a], dest(0, way), way) if first else landed.at[step - 1, k]
        return pltpu.make_async_remote_copy(
            src_ref=source,
            dst_ref=landed.at[step, k],
            send_sem=sum_send.at[step, k],
            recv_sem=sum_recv.at[step, k],
            device_id={"dp": peers[way]},
            device_id_type=pl.DeviceIdType.MESH,
        )

    def own_copy(step, way, a):
        k = 2 * a + way
        place = block(outs[a], me - step if way == 0 else me + step, way)
        return pltpu.make_async_remote_copy(
            src_ref=place,
            dst_ref=place,
            send_sem=own_send.at[step, k],
            recv_sem=own_recv.at[step, k],
            device_id={"dp": peers[way]},
            device_id_type=pl.DeviceIdType.MESH,
        )

    def own_arrival(step, way, a):
        k = 2 * a + way
        place = block(outs[a], me - 1 - step if way == 0 else me + 1 + step, way)
        return pltpu.make_async_remote_copy(
            src_ref=place,
            dst_ref=place,
            send_sem=own_send.at[step, k],
            recv_sem=own_recv.at[step, k],
            device_id={"dp": peers[way]},
            device_id_type=pl.DeviceIdType.MESH,
        )

    def total(step, way, a):
        mine = block(partials[a], dest(step + 1, way), way)[...].astype(jnp.float32)
        return landed[step, 2 * a + way].astype(jnp.float32) + mine

    barrier = pltpu.get_barrier_semaphore()
    for peer in peers:
        pl.semaphore_signal(
            barrier, inc=1, device_id={"dp": peer}, device_id_type=pl.DeviceIdType.MESH
        )
    pl.semaphore_wait(barrier, 2)

    for way, a in streams:
        sum_copy(0, way, a, True).start()

    def sum_forward(step, way, a):
        sum_copy(step, way, a, True).wait_recv()
        landed[step, 2 * a + way] = total(step, way, a).astype(jnp.bfloat16)
        sum_copy(step + 1, way, a).start()

    def own_forward(step, way, a):
        own_arrival(step, way, a).wait_recv()
        own_copy(step + 1, way, a).start()

    def drain(step, way, a):
        sum_copy(step, way, a, True).wait_send()
        own_copy(step, way, a).wait_send()

    def run(act, less):
        def both(step, carry):
            for way, a in streams:
                act(step, way, a)
            return carry

        lax.fori_loop(0, hops[1] - less, both, 0)
        for step in range(hops[1] - less, hops[0] - less):
            for a in range(3):
                act(step, 0, a)

    run(sum_forward, 1)
    values = []
    for a in range(3):
        sum_copy(hops[0] - 1, 0, a, True).wait_recv()
        sum_copy(hops[1] - 1, 1, a, True).wait_recv()
        values.append(
            total(hops[0] - 1, 0, a) + landed[hops[1] - 1, 2 * a + 1].astype(jnp.float32)
        )
    for a, value in enumerate(pointwise(*values)):
        block(outs[a], me, 0)[...] = value
    for way, a in streams:
        own_copy(0, way, a).start()
    run(own_forward, 1)
    for way, a in streams:
        own_arrival(hops[way] - 1, way, a).wait_recv()
    run(drain, 0)


def reduced_units(partials):
    ring = lax.axis_size("dp")
    rows, units = partials[0].shape
    sems = pltpu.SemaphoreType.DMA((ring // 2, 6))
    return pl.pallas_call(
        functools.partial(ring_kernel, ring),
        out_shape=[jax.ShapeDtypeStruct((rows, units), jnp.bfloat16)] * 3,
        in_specs=[pl.BlockSpec(memory_space=pltpu.VMEM)] * 3,
        out_specs=[pl.BlockSpec(memory_space=pltpu.VMEM)] * 3,
        scratch_shapes=[
            pltpu.VMEM((ring // 2, 6, rows // ring, units), jnp.bfloat16),
            sems,
            sems,
            sems,
            sems,
        ],
        compiler_params=pltpu.CompilerParams(
            collective_id=0, has_side_effects=True, vmem_limit_bytes=48 * 1024 * 1024
        ),
    )(*partials)


def shards(tokens, route_ids, route_weights, gate_weight, up_weight, down_weight, out_grad):
    expert_count = lax.axis_size("expert")
    tok_count, width = tokens.shape
    top_count = route_ids.shape[1]
    capacity = min(tok_count, tok_count * top_count // expert_count + tok_count // 16)
    weight_g, weight_u, weight_d = gate_weight[0], up_weight[0], down_weight[0]
    place, scale = slot_matrices(route_ids, route_weights, expert_count, capacity)
    chunks, start = [], 0
    for size in SLOT_CHUNKS:
        chunks.append(
            tuple(
                m[:, start : start + size].reshape(expert_count * size, tok_count)
                for m in (place, scale)
            )
        )
        start += size
    assert start == capacity
    sent = []
    for place_c, scale_c in chunks:
        sent.append(
            swap(
                jnp.concatenate(
                    [
                        dot_of(place_c, tokens, 1, 0).astype(jnp.bfloat16),
                        dot_of(scale_c, out_grad, 1, 0).astype(jnp.bfloat16),
                    ],
                    axis=1,
                )
            )
        )
    parts, after = [], None
    for got in sent:
        if after is not None and False:
            got, after = lax.optimization_barrier((got, after))
            parts[-1] = parts[-1][:3] + after
        rows, upstream = got[:, :width], got[:, width:]
        partial = (
            dot_of(rows, weight_g, 1, 0).astype(jnp.bfloat16),
            dot_of(rows, weight_u, 1, 0).astype(jnp.bfloat16),
            dot_of(upstream, weight_d, 1, 1).astype(jnp.bfloat16),
        )
        after = reduced_units(partial)
        parts.append((rows, upstream, None) + tuple(after))
    mixed = input_grad = gate_grad = up_grad = down_grad = 0.0
    for (place_c, scale_c), (rows, upstream, _, *summed) in zip(chunks, parts):
        hidden, gate_delta, up_delta = summed
        produced = dot_of(hidden, weight_d, 1, 0).astype(jnp.bfloat16)
        back_rows = (
            dot_of(gate_delta, weight_g, 1, 1) + dot_of(up_delta, weight_u, 1, 1)
        ).astype(jnp.bfloat16)
        back = swap(jnp.concatenate([produced, back_rows], axis=1))
        mixed += dot_of(scale_c, back[:, :width], 0, 0)
        input_grad += dot_of(place_c, back[:, width:], 0, 0)
        gate_grad += dot_of(rows, gate_delta, 0, 0)
        up_grad += dot_of(rows, up_delta, 0, 0)
        down_grad += dot_of(hidden, upstream, 0, 0)
    return (
        mixed.astype(jnp.bfloat16),
        input_grad.astype(jnp.bfloat16),
        gate_grad[None],
        up_grad[None],
        down_grad[None],
    )


def solution(mesh):
    return jax.shard_map(
        shards,
        mesh=mesh,
        in_specs=(
            P("expert", "dp"),
            P("expert", None),
            P("expert", None),
            P("expert", "dp", None),
            P("expert", "dp", None),
            P("expert", None, "dp"),
            P("expert", "dp"),
        ),
        out_specs=(
            P("expert", "dp"),
            P("expert", "dp"),
            P("expert", "dp", None),
            P("expert", "dp", None),
            P("expert", None, "dp"),
        ),
        check_vma=False,
    )
```
